32 devices in a mesh: ctx: 16 (over z, y, x), head: 2 (over core).
Axes of the slice: x: 2, y: 2, z: 4, core: 2. Of those that a mesh axis runs over, the one named last changes fastest.
Arguments:
- score_grad: bfloat16 [16384, 768], P('ctx'), may hold values from -6 to 6
- queries: bfloat16 [768, 64, 128], P('ctx', 'head'), may hold values from -1 to 1, as said below
- head_weights: bfloat16 [768, 64], P('ctx', 'head'), may hold values from -0.75 to 0.75
- keys: bfloat16 [16384, 128], P('ctx'), may hold values from -1 to 1, as said below
- positions: int32 [768], replicated, may hold values from 0 to 16383, as said below
Outputs:
- query_grad: float32 [768, 64, 128], P('ctx', 'head')
- weight_grad: float32 [768, 64], P('ctx', 'head')
- key_grad: float32 [16384, 128], P('ctx')
The draws below stay inside these ranges and needn't reach their ends.
Inputs may be any that keep to these rules, and one draw needn't show every extreme that they name: positions rise with the query index; query t has a position from t * 16384 // 768 to (t + 1) * 16384 // 768 - 1. `queries`: entries are multiples of 1 / 256. `keys`: entries are multiples of 1 / 256.
All inputs are finite; a program needn't handle non-finite values.
Results may differ from the reference program's by a relative error of at most 0.0055.
Values may be sent and summed in bfloat16 or wider, within the bound.
No kernel may reach another device: no remote copies, remote signals or barrier semaphores. Data moves between devices by JAX's collectives and lax.ppermute only.
A program may use at most 64 MiB of HBM per device.

```python
import jax
import jax.numpy as jnp
from jax import lax

DH = 128
HEADS = 64
QUERIES = 768
KEYS = 16384


def draw_positions(key, part):
    index = jnp.arange(QUERIES, dtype=jnp.int32)
    lower = index * KEYS // QUERIES
    upper = (index + 1) * KEYS // QUERIES
    return lower + jax.random.randint(key, (QUERIES,), 0, upper - lower, dtype=jnp.int32)


def grid_values(key, shape):
    first = jax.random.fold_in(key, 11)
    return jax.random.randint(first, shape, -40, 41, dtype=jnp.int32).astype(jnp.float32) / 64.0


def draw_queries(key, part):
    return grid_values(key, (QUERIES, HEADS, DH)).astype(jnp.bfloat16)


def draw_keys(key, part):
    return grid_values(key, (KEYS, DH)).astype(jnp.bfloat16)


def block_scale(rng, extent, pieces, smallest, top_value):
    def one(axis_at, shards_of):
        heights = jax.random.uniform(jax.random.fold_in(jax.random.fold_in(rng, 6), axis_at), (shards_of,), jnp.float32, smallest / len(pieces), top_value / len(pieces))
        return jnp.repeat(jnp.exp(heights), extent[axis_at] // shards_of).reshape((-1,) + (1,) * (len(extent) - axis_at - 1))

    gain = one(*pieces[0])
    for cut in pieces[1:]:
        gain = gain * one(*cut)
    return gain


def bell_draw(key, shape, scale, limit, split=(), kind=jnp.bfloat16):
    level = block_scale(key, shape, split, -0.22, 0.18) if split else 1.0
    result = jax.random.normal(key, shape, jnp.float32) * scale * level
    return jnp.minimum(jnp.maximum(result, -limit), limit).astype(kind)


def setup_inputs(seed: int = 0) -> dict:
    streams_of = jax.random.split(jax.random.key(seed), 6)
    return {
        "score_grad": bell_draw(streams_of[0], (KEYS, QUERIES), 1.0, 6.0, ((0, 16),)),
        "queries": draw_queries(jax.random.fold_in(streams_of[5], 71), 0),
        "head_weights": bell_draw(streams_of[2], (QUERIES, HEADS), 0.125, 0.75, ((0, 16), (1, 2))),
        "keys": draw_keys(jax.random.fold_in(streams_of[5], 71), 0),
        "positions": draw_positions(jax.random.fold_in(streams_of[5], 71), 0),
    }


def tile_terms(key_rows, grad_rows, key_place, query_rows, weight_rows, query_place, scale):
    heads = weight_rows.shape[1]
    key_count = key_rows.shape[0]
    query_count = weight_rows.shape[0]
    scores = lax.dot_general(key_rows, query_rows, (((1,), (1,)), ((), ())), preferred_element_type=jnp.float32)
    scores = scores.reshape(key_count, query_count, heads)
    active = jnp.maximum(scores, 0.0)
    opened = jnp.where(scores > 0.0, jnp.ones((), jnp.float32), jnp.zeros((), jnp.float32))
    visible = key_place[:, None] <= query_place[None, :]
    masked = jnp.where(visible, grad_rows.astype(jnp.float32), jnp.zeros((), jnp.float32))
    weight_add = scale * jnp.einsum("sq,sqh->qh", masked, active)
    coef = (masked[:, :, None] * weight_rows[None, :, :] * opened * scale).astype(jnp.bfloat16)
    coef = coef.reshape(key_count, query_count * heads)
    query_add = lax.dot_general(coef, key_rows, (((0,), (0,)), ((), ())), preferred_element_type=jnp.float32)
    key_add = jnp.dot(coef, query_rows, preferred_element_type=jnp.float32)
    return query_add, weight_add, key_add


def sweep(key_rows, grad_rows, key_place, flat_queries, weights, positions, scale, query_acc, weight_acc):
    heads = weights.shape[1]
    total = weights.shape[0]
    qblock = min(128, total)
    turns = total // qblock
    lowest = jnp.min(key_place)

    def turn(index, carry):
        start = (index * qblock).astype(jnp.int32)
        query_place = lax.dynamic_slice_in_dim(positions, start, qblock)

        def work(state):
            query_state, weight_state, key_state = state
            query_rows = lax.dynamic_slice_in_dim(flat_queries, start * heads, qblock * heads)
            weight_rows = lax.dynamic_slice_in_dim(weights, start, qblock)
            grad_block = lax.dynamic_slice_in_dim(grad_rows, start, qblock, 1)
            query_add, weight_add, key_add = tile_terms(key_rows, grad_block, key_place, query_rows, weight_rows, query_place, scale)
            older = lax.dynamic_slice_in_dim(query_state, start * heads, qblock * heads)
            query_state = lax.dynamic_update_slice_in_dim(query_state, older + query_add, start * heads, 0)
            older_weight = lax.dynamic_slice_in_dim(weight_state, start, qblock)
            weight_state = lax.dynamic_update_slice_in_dim(weight_state, older_weight + weight_add, start, 0)
            return query_state, weight_state, key_state + key_add

        def skip(state):
            return state

        return lax.cond(jnp.max(query_place) >= lowest, work, skip, carry)

    key_zero = jnp.zeros((key_rows.shape[0], flat_queries.shape[1]), jnp.float32)
    return lax.fori_loop(0, turns, turn, (query_acc, weight_acc, key_zero))


def reference(score_grad, queries, head_weights, keys, positions):
    total, heads, width = queries.shape
    scale = float(width) ** -0.5
    flat = queries.reshape(total * heads, width)
    weights = head_weights.astype(jnp.float32)
    key_total = keys.shape[0]
    kblock = min(512, key_total)
    blocks = key_total // kblock
    places = jnp.arange(key_total, dtype=jnp.int32)

    def advance(carry, index):
        query_acc, weight_acc = carry
        start = (index * kblock).astype(jnp.int32)
        key_rows = lax.dynamic_slice_in_dim(keys, start, kblock)
        grad_rows = lax.dynamic_slice_in_dim(score_grad, start, kblock)
        key_place = lax.dynamic_slice_in_dim(places, start, kblock)
        query_acc, weight_acc, key_add = sweep(key_rows, grad_rows, key_place, flat, weights, positions, scale, query_acc, weight_acc)
        return (query_acc, weight_acc), key_add

    init = (jnp.zeros((total * heads, width), jnp.float32), jnp.zeros((total, heads), jnp.float32))
    (query_acc, weight_acc), key_parts = lax.scan(advance, init, jnp.arange(blocks, dtype=jnp.int32))
    return query_acc.reshape(total, heads, width), weight_acc, key_parts.reshape(key_total, width)
```

```python
import functools

import jax
import jax.numpy as jnp
from jax import lax
from jax.experimental import pallas as pl
from jax.experimental.pallas import tpu as pltpu
from jax.sharding import PartitionSpec as P


BF16 = jnp.bfloat16
F32 = jnp.float32
AXES = ("ctx", "head")


def round_up(value, unit):
    return (value + unit - 1) // unit * unit


def full_spec(array):
    rank = len(array.shape)
    return pl.BlockSpec(array.shape, lambda *_: (0,) * rank)


def call(kernel, inputs, outputs, scratch=(), aliases=None, flops=0):
    specs = [pl.BlockSpec(memory_space=pltpu.SMEM)] + [full_spec(x) for x in inputs[1:]]
    total = sum(x.size * x.dtype.itemsize for x in inputs) + sum(
        x.size * x.dtype.itemsize for x in outputs
    )
    return pl.pallas_call(
        kernel,
        in_specs=specs,
        out_specs=[full_spec(x) for x in outputs],
        out_shape=list(outputs),
        scratch_shapes=list(scratch),
        input_output_aliases=aliases or {},
        cost_estimate=pl.CostEstimate(flops=flops, transcendentals=0, bytes_accessed=total),
        compiler_params=pltpu.CompilerParams(vmem_limit_bytes=56 << 20),
    )(*inputs)


class Plan:
    def __init__(self, mesh, queries, keys):
        self.ranks = mesh.shape["ctx"]
        self.cores = mesh.shape["head"]
        self.lanes = 4 if self.ranks % 4 == 0 else 1
        self.line = self.ranks // self.lanes
        self.count = queries.shape[0]
        self.heads = queries.shape[1]
        self.width = queries.shape[2]
        self.slots = round_up(self.count, 16)
        self.rows = self.slots * self.heads
        self.wrows = round_up(-(-self.rows // self.width), 16)
        self.keys = keys.shape[0]
        self.piece = self.keys // self.cores
        self.band = self.lanes * self.slots
        self.scale = float(self.width) ** (-0.5)

    def swap_lane(self, offset):
        return [
            (self.flat(rank, core), self.flat(rank ^ offset, core))
            for rank in range(self.ranks)
            for core in range(self.cores)
        ]

    def swap_core(self, offset):
        return [
            (self.flat(rank, core), self.flat(rank, core ^ offset))
            for rank in range(self.ranks)
            for core in range(self.cores)
        ]

    def shift_up(self, step):
        return [
            (self.flat(rank, core), self.flat(rank + step * self.lanes, core))
            for rank in range(self.ranks - step * self.lanes)
            for core in range(self.cores)
        ]

    def shift_down(self, step):
        return [(there, here) for here, there in self.shift_up(step)]

    def flat(self, rank, core):
        return rank * self.cores + core


def prepare_kernel(plan, where, grads, keys, place, flat, weights, *refs):
    line, cores = plan.line, plan.cores
    locals_out = refs[:cores]
    sends_out = refs[cores : cores + line - 1]
    packed_out = refs[cores + line - 1]
    turned, turned_keys = refs[cores + line :]
    z, core = where[0], where[2]
    width, piece, band = plan.width, plan.piece, plan.band
    packed_out[pl.ds(0, plan.rows), :] = flat[...]
    packed_out[pl.ds(plan.rows, plan.wrows), :] = weights[...]
    for part in range(cores):
        rows = pl.ds(part * piece, piece)
        turned_keys[part] = keys[rows, :].T
        turned[part] = grads[rows, :].T
    for offset in range(cores):
        part = jnp.bitwise_xor(core, offset)
        out = locals_out[offset]
        out[pl.ds(0, width), :] = turned_keys[part]
        block = turned[part, pl.ds(pl.multiple_of(z * band, 16), band), :]
        first = (z * plan.lanes + where[1]) * plan.keys + part * piece
        spot = first + lax.broadcasted_iota(jnp.int32, (band, piece), 1)
        seen = spot <= place[...]
        kept = jnp.where(seen, block.astype(F32), jnp.zeros((), F32)).astype(BF16)
        out[pl.ds(width, band), :] = kept
    for step in range(1, line):
        @pl.when(z + step < line)
        def _(step=step):
            out = sends_out[step - 1]
            out[pl.ds(0, width), :] = turned_keys[core]
            out[pl.ds(width, band), :] = turned[
                core, pl.ds(pl.multiple_of((z + step) * band, 16), band), :
            ]


def prepare(plan, where, grads, keys, place, flat, weights):
    total = plan.ranks * plan.slots
    shape = (plan.width + plan.band, plan.piece)
    outputs = [jax.ShapeDtypeStruct(shape, BF16)] * (plan.cores + plan.line - 1)
    outputs.append(jax.ShapeDtypeStruct((plan.rows + plan.wrows, plan.width), BF16))
    found = call(
        functools.partial(prepare_kernel, plan),
        [where, grads, keys, place, flat, weights],
        outputs,
        [
            pltpu.VMEM((plan.cores, total, plan.piece), BF16),
            pltpu.VMEM((plan.cores, plan.width, plan.piece), BF16),
        ],
    )
    cut = plan.cores + plan.line - 1
    return found[: plan.cores], found[plan.cores : cut], found[cut]


def sweep_kernel(plan, blocks, steps, more_queries, more_keys, where, *refs):
    refs = list(refs)

    def take(number):
        found = refs[:number]
        del refs[:number]
        return found

    pieces = len(steps) * plan.cores
    packs = take(len(blocks))
    parts = take(pieces)
    query_in = take(len(blocks) if more_queries else 0)
    key_in = take(pieces if more_keys else 0)
    query_out = take(len(blocks))
    key_out = take(pieces)
    sums = take(len(blocks))
    scaled = take(len(blocks))
    z, lane = where[0], where[1]
    width = plan.width
    tile = min(plan.slots, 16)
    group = tile * plan.heads
    for spot, pack in enumerate(packs):
        lines = plan.rows // width
        row = jnp.concatenate(
            [pack[pl.ds(plan.rows + i, 1), :] for i in range(lines)], axis=1
        ).astype(F32)
        turned = pack[pl.ds(0, plan.rows), :].T.astype(F32)
        scaled[spot][...] = (turned * (row * plan.scale)).astype(BF16)
        sums[spot][...] = query_in[spot][...] if more_queries else jnp.zeros_like(sums[spot])
    for spot in range(pieces):
        key_out[spot][...] = key_in[spot][...] if more_keys else jnp.zeros_like(key_out[spot])
    for index, step in enumerate(steps):
        for spot, block in enumerate(blocks):
            other = jnp.bitwise_xor(lane, block)
            fits = (other >= lane) if step == 0 else (z >= step)

            @pl.when(fits)
            def _(index=index, spot=spot, other=other):
                base = pl.multiple_of(width + other * plan.slots, 16)
                for core in range(plan.cores):
                    part = parts[index * plan.cores + core]
                    total = key_out[index * plan.cores + core]
                    turned = part[pl.ds(0, width), :]
                    added = total[...]
                    for turn in range(plan.slots // tile):
                        rows = pl.ds(turn * group, group)
                        scores = jnp.dot(
                            packs[spot][rows, :], turned, preferred_element_type=F32
                        )
                        masked = part[pl.ds(base + turn * tile, tile), :]
                        if plan.heads % 16 == 0:
                            spread = jnp.broadcast_to(
                                masked[:, None, :], (tile, plan.heads, plan.piece)
                            ).reshape(group, plan.piece)
                            gate = jnp.where(
                                scores.astype(BF16) > 0, spread, jnp.zeros((), BF16)
                            )
                        else:
                            spread = jnp.broadcast_to(
                                masked.astype(F32)[:, None, :], (tile, plan.heads, plan.piece)
                            ).reshape(group, plan.piece)
                            gate = jnp.where(scores > 0, spread, jnp.zeros((), F32)).astype(BF16)
                        sums[spot][rows, :] += lax.dot_general(
                            gate, turned, (((1,), (1,)), ((), ())), preferred_element_type=F32
                        )
                        added = added + jnp.dot(
                            scaled[spot][:, rows], gate, preferred_element_type=F32
                        )
                    total[...] = added
    for spot in range(len(blocks)):
        query_out[spot][...] = sums[spot][...].astype(query_out[spot].dtype)


def sweep(plan, where, blocks, steps, packs, parts, query_in, key_in, query_type):
    more_queries, more_keys = query_in is not None, key_in is not None
    inputs = [where] + list(packs) + list(parts)
    if more_queries:
        inputs += list(query_in)
    if more_keys:
        inputs += list(key_in)
    pieces = len(steps) * plan.cores
    query_out = [jax.ShapeDtypeStruct((plan.rows, plan.width), query_type)] * len(blocks)
    key_out = [jax.ShapeDtypeStruct((plan.width, plan.piece), F32)] * pieces
    scratch = [pltpu.VMEM((plan.rows, plan.width), F32)] * len(blocks)
    scratch += [pltpu.VMEM((plan.width, plan.rows), BF16)] * len(blocks)
    flops = 6 * plan.rows * plan.piece * plan.width * pieces * len(blocks)
    found = call(
        functools.partial(sweep_kernel, plan, blocks, steps, more_queries, more_keys),
        inputs,
        query_out + key_out,
        scratch,
        flops=flops,
    )
    return found[: len(blocks)], found[len(blocks) :]


def local(mesh, score_grad, queries, head_weights, keys, positions):
    plan = Plan(mesh, queries, keys)
    rank, core = lax.axis_index("ctx"), lax.axis_index("head")
    z, lane = rank // plan.lanes, rank % plan.lanes
    where = jnp.stack([z, lane, core]).astype(jnp.int32)
    extra = plan.slots - plan.count
    place = lax.dynamic_slice_in_dim(
        positions, z * plan.lanes * plan.count, plan.lanes * plan.count
    )
    grads, flat, weights = score_grad, queries, head_weights
    if extra:
        grads = grads.reshape(plan.keys, plan.ranks, plan.count)
        grads = jnp.pad(grads, ((0, 0), (0, 0), (0, extra))).reshape(plan.keys, -1)
        flat = jnp.pad(flat, ((0, extra), (0, 0), (0, 0)))
        weights = jnp.pad(weights, ((0, extra), (0, 0)))
        place = jnp.pad(
            place.reshape(plan.lanes, plan.count), ((0, 0), (0, extra)), constant_values=-1
        ).reshape(-1)
    flat = flat.reshape(plan.rows, plan.width)
    weights = weights.reshape(-1, plan.width)
    weights = jnp.pad(weights, ((0, plan.wrows - weights.shape[0]), (0, 0)))
    here, sends, pack = prepare(
        plan, where, grads, keys, place.reshape(plan.band, 1), flat, weights
    )

    def move(array, pairs):
        return lax.ppermute(array, AXES, pairs)

    packs = [pack] + [move(pack, plan.swap_lane(j)) for j in range(1, plan.lanes)]
    chunks = [list(here)]
    for step in range(1, plan.line):
        mine = move(sends[step - 1], plan.shift_up(step))
        chunks.append([mine] + [move(mine, plan.swap_core(j)) for j in range(1, plan.cores)])

    others = list(range(1, plan.lanes))
    own_sum, key_sums = None, [None] * plan.line
    early = list(range(min(2, plan.line)))
    late = list(range(len(early), plan.line))
    for step in early:
        own_sum, key_sums[step] = sweep(
            plan, where, [0], [step], [packs[0]], chunks[step], own_sum, None, F32
        )
    sums = None
    for step in range(plan.line):
        last = step == plan.line - 1
        if others:
            sums, key_sums[step] = sweep(
                plan, where, others, [step], packs[1:], chunks[step], sums, key_sums[step],
                BF16 if last else F32,
            )
    arrived = [move(part, plan.swap_lane(j)) for j, part in zip(others, sums or [])]
    for step in late:
        own_sum, key_sums[step] = sweep(
            plan, where, [0], [step], [packs[0]], chunks[step], own_sum, key_sums[step], F32
        )

    def join_cores(parts, kind):
        total = parts[0]
        for offset in range(1, plan.cores):
            total = total + move(parts[offset].astype(kind), plan.swap_core(offset)).astype(F32)
        return total

    half = join_cores(key_sums[0], F32)
    for step in range(1, plan.line):
        outgoing = join_cores(key_sums[step], BF16).astype(BF16)
        half = half + move(outgoing, plan.shift_down(step)).astype(F32)
    half = half.T
    shares = [half] + [move(half, plan.swap_core(j)) for j in range(1, plan.cores)]
    stacked = jnp.stack(shares)
    key_grad = jnp.concatenate(
        [
            lax.dynamic_index_in_dim(stacked, jnp.bitwise_xor(core, j), 0, keepdims=False)
            for j in range(plan.cores)
        ],
        0,
    )
    total = own_sum[0]
    for part in arrived:
        total = total + part.astype(F32)
    total = total.reshape(plan.slots, plan.heads, plan.width)[: plan.count]
    gain = head_weights.astype(F32) * plan.scale
    query_grad = total * gain[:, :, None]
    weight_grad = plan.scale * jnp.sum(total * queries.astype(F32), axis=-1)
    return (query_grad, weight_grad, key_grad)


def solution(mesh):
    placed = (P("ctx", None), P("ctx", "head", None), P("ctx", "head"), P("ctx", None), P())
    return jax.shard_map(
        functools.partial(local, mesh),
        mesh=mesh,
        in_specs=placed,
        out_specs=(P("ctx", "head", None), P("ctx", "head"), P("ctx", None)),
        check_vma=False,
    )
```
